32 devices in a mesh: angle: 4 (over y, x), panel: 8 (over z, core).
Axes of the slice: x: 2, y: 2, z: 4, core: 2. Of those that a mesh axis runs over, the one named last changes fastest.
Arguments:
- measured: bfloat16 [64, 512, 1024], P(('angle', 'panel')), may hold values from 0.099609375 to 1
- predicted: bfloat16 [64, 512, 1024], P(('angle', 'panel')), may hold values from 0 to 2
- slice_filter: bfloat16 [512, 512], replicated, may hold values from -0.25 to 0.25
- column_filter: bfloat16 [1024, 1024], replicated, may hold values from -0.1875 to 0.1875
- volume: float32 [512, 16384], P('angle', 'panel'), may hold values from 0 to 1
- tiles: bfloat16 [1536, 128, 128], P('panel'), may hold values from -0.5 to 0.5
- tile_ray: int32 [1536], P('panel'), may hold values from 0 to 63
- tile_vox: int32 [1536], P('panel'), may hold values from 0 to 127
- live_tiles: int32 [8], P('panel'), may hold values from 1 to 192, as said below
Outputs:
- updated_volume: float32 [512, 16384], P('angle', 'panel')
- projected: bfloat16 [64, 512, 1024], P(('angle', 'panel'))
The draws below stay inside these ranges and needn't reach their ends.
Inputs may be any that keep to these rules, and one draw needn't show every extreme that they name: live_tiles[p] counts the tile slots of panel p that are used, from the first slot on; at least one panel uses all 192 slots.
All inputs are finite; a program needn't handle non-finite values.
Results may differ from the reference program's by a relative error of at most 0.0065.
Values may be sent and summed in bfloat16 or wider, within the bound.
No kernel may reach another device: no remote copies, remote signals or barrier semaphores. Data moves between devices by JAX's collectives and lax.ppermute only.
A program may use at most 128 MiB of HBM per device.

```python
import jax
import jax.numpy as jnp
import numpy as np
from jax import lax

NCOL = 1024
SL = 512
A_DEV = 2
TILES = 192
ANGLES = 64
NV = 16384
RAYB = 64
VB = 128
N_ANGLE = 4
N_PANEL = 8


def draw_live_tiles(key, part):
    counts = jax.random.randint(jax.random.fold_in(key, 11), (N_PANEL,), max(1, TILES // 4), TILES + 1)
    fullest = jax.random.randint(jax.random.fold_in(key, 12), (), 0, N_PANEL)
    return jnp.where(jnp.arange(N_PANEL) == fullest, TILES, counts).astype(jnp.int32)


def with_ends(values, stream_key, least, largest):
    dims = values.shape
    place = [jax.random.randint(jax.random.fold_in(stream_key, axis), (), 0, dims[axis]) for axis in range(len(dims))]
    values = values.at[tuple(place)].set(least)
    longest = dims.index(max(dims))
    place[longest] = (place[longest] + 1) % dims[longest]
    return values.at[tuple(place)].set(largest)


def steps_of(own_key, shape, split, smallest, largest):
    def one(axis_at, shards_of):
        steps = jax.random.uniform(jax.random.fold_in(jax.random.fold_in(own_key, 6), axis_at), (shards_of,), jnp.float32, smallest / len(split), largest / len(split))
        return jnp.repeat(jnp.exp(steps), shape[axis_at] // shards_of).reshape((-1,) + (1,) * (len(shape) - axis_at - 1))

    level = one(*split[0])
    for cut in split[1:]:
        level = level * one(*cut)
    return level


def centred(key, shape, spread, limit, shards=(), held_as=jnp.bfloat16):
    level = steps_of(key, shape, shards, -0.22, 0.18) if shards else 1.0
    values = jax.random.normal(key, shape, jnp.float32) * spread * level
    return jnp.minimum(jnp.maximum(values, -limit), limit).astype(held_as)


def setup_inputs(seed: int = 0) -> dict:
    streams_of = jax.random.split(jax.random.key(seed), 10)
    measured = jnp.clip(0.099609375 + 0.9003906 * jax.random.uniform(streams_of[0], (ANGLES, SL, NCOL), jnp.float32) ** steps_of(streams_of[0], (ANGLES, SL, NCOL), ((0, 32),), -0.2, 0.2), 0.099609375, 1.0).astype(jnp.bfloat16)
    predicted = jnp.clip(2.0 * jax.random.uniform(streams_of[1], (ANGLES, SL, NCOL), jnp.float32) ** steps_of(streams_of[1], (ANGLES, SL, NCOL), ((0, 32),), -0.2, 0.2), 0.0, 2.0).astype(jnp.bfloat16)
    slice_filter = centred(streams_of[2], (SL, SL), SL ** -0.5, 0.25)
    column_filter = centred(streams_of[3], (NCOL, NCOL), NCOL ** -0.5, 0.1875)
    volume = jnp.clip(1.0 * jax.random.uniform(streams_of[4], (SL, NV), jnp.float32) ** steps_of(streams_of[4], (SL, NV), ((0, 4), (1, 8)), -0.2, 0.2), 0.0, 1.0)
    tiles = centred(streams_of[5], (N_PANEL * TILES, 128, 128), 128 ** -0.5, 0.5, ((0, 8),))
    tile_ray = with_ends(jax.random.randint(streams_of[6], (N_PANEL * TILES,), 0, RAYB), jax.random.fold_in(streams_of[6], 1), 0, RAYB - 1).astype(jnp.int32)
    tile_vox = with_ends(jax.random.randint(streams_of[7], (N_PANEL * TILES,), 0, VB), jax.random.fold_in(streams_of[7], 1), 0, VB - 1).astype(jnp.int32)
    live_tiles = draw_live_tiles(jax.random.fold_in(streams_of[9], 71), 0)
    return {"measured": measured, "predicted": predicted, "slice_filter": slice_filter, "column_filter": column_filter, "volume": volume, "tiles": tiles, "tile_ray": tile_ray, "tile_vox": tile_vox, "live_tiles": live_tiles}


step_size = 0.1


def panel_angles(panel):
    listed = [(outer * N_PANEL + panel) * A_DEV + inner for outer in range(N_ANGLE) for inner in range(A_DEV)]
    return jnp.asarray(np.array(listed, dtype=np.int32))


def reference(measured, predicted, slice_filter, column_filter, volume, tiles, tile_ray, tile_vox, live_tiles):
    bright = jnp.exp(-predicted.astype(jnp.float32))
    misfit = ((measured.astype(jnp.float32) - bright) * bright).astype(jnp.bfloat16)
    across = jnp.dot(misfit.reshape(-1, NCOL), column_filter, preferred_element_type=jnp.float32)
    across = across.astype(jnp.bfloat16).reshape(misfit.shape)
    filtered = lax.map(lambda angle_plane: jnp.dot(slice_filter, angle_plane, preferred_element_type=jnp.float32).astype(jnp.bfloat16), across)
    col_blocks = NCOL // 128
    voxel_blocks = NV // 128
    local_angles = A_DEV * N_ANGLE
    gradient = jnp.zeros((SL, voxel_blocks, 128), jnp.float32)
    for panel in range(N_PANEL):
        angles = panel_angles(panel)
        ray_grid = filtered[angles].reshape(local_angles, SL, col_blocks, 128)
        ray_ids = tile_ray[panel * TILES:(panel + 1) * TILES].astype(jnp.int32)
        vox_ids = tile_vox[panel * TILES:(panel + 1) * TILES].astype(jnp.int32)
        panel_tiles = tiles[panel * TILES:(panel + 1) * TILES].astype(jnp.float32)
        active = jnp.arange(TILES) < live_tiles[panel]
        picked = ray_grid[ray_ids // col_blocks, :, ray_ids % col_blocks, :].astype(jnp.float32)
        contrib = jnp.einsum('tsr,trv->stv', picked, panel_tiles)
        contrib = jnp.where(active[None, :, None], contrib, jnp.float32(0.0))
        gradient = gradient.at[:, vox_ids, :].add(contrib)
    updated = jnp.clip(volume + step_size * gradient.reshape(SL, NV), 0.0, 1.0)
    voxels = updated.astype(jnp.bfloat16).reshape(SL, voxel_blocks, 128)
    projected = jnp.zeros((ANGLES, SL, NCOL), jnp.bfloat16)
    for panel in range(N_PANEL):
        angles = panel_angles(panel)
        ray_ids = tile_ray[panel * TILES:(panel + 1) * TILES].astype(jnp.int32)
        vox_ids = tile_vox[panel * TILES:(panel + 1) * TILES].astype(jnp.int32)
        panel_tiles = tiles[panel * TILES:(panel + 1) * TILES].astype(jnp.float32)
        active = jnp.arange(TILES) < live_tiles[panel]
        picked = voxels[:, vox_ids, :].astype(jnp.float32)
        contrib = jnp.einsum('stv,trv->tsr', picked, panel_tiles)
        contrib = jnp.where(active[:, None, None], contrib, jnp.float32(0.0))
        summed = jnp.zeros((local_angles, SL, col_blocks, 128), jnp.float32)
        summed = summed.at[ray_ids // col_blocks, :, ray_ids % col_blocks, :].add(contrib)
        projected = projected.at[angles].set(summed.astype(jnp.bfloat16).reshape(local_angles, SL, NCOL))
    return updated, projected
```

```python
import functools

import jax
import jax.numpy as jnp
from jax import lax
from jax.experimental import pallas as pl
from jax.experimental.pallas import tpu as pltpu
from jax.sharding import PartitionSpec as P

step_size = 0.1
LANES = 128
UNROLL = 8
CHUNKS = 2
VMEM_LIMIT = 50 * 1024 * 1024


VMEM_SPEC = pl.BlockSpec(memory_space=pltpu.VMEM)
ANY_SPEC = pl.BlockSpec(memory_space=pl.ANY)
SMEM_SPEC = pl.BlockSpec(memory_space=pltpu.SMEM)


def params():
    return pltpu.CompilerParams(vmem_limit_bytes=VMEM_LIMIT)


def swap(value, axis, mask):
    size = lax.axis_size(axis)
    return lax.ppermute(value, axis, [(i, i ^ mask) for i in range(size)])


def filter_rows(slice_ref, start_ref, across, outs, angle, rows):
    picked = jnp.concatenate(
        [slice_ref[pl.ds(pl.multiple_of(start_ref[m], rows), rows), :] for m in range(len(outs))], axis=0
    )
    result = jnp.dot(picked, across, preferred_element_type=jnp.float32).astype(jnp.bfloat16)
    for m, out in enumerate(outs):
        out[angle] = result[m * rows : (m + 1) * rows]


def first_filter_kernel(rows, start_ref, measured, predicted, slice_ref, column_ref, across_out, *outs):
    for angle in range(measured.shape[0]):
        bright = jnp.exp(-predicted[angle].astype(jnp.float32))
        misfit = ((measured[angle].astype(jnp.float32) - bright) * bright).astype(jnp.bfloat16)
        across = jnp.dot(misfit, column_ref[...], preferred_element_type=jnp.float32).astype(jnp.bfloat16)
        across_out[angle] = across
        filter_rows(slice_ref, start_ref, across, outs, angle, rows)


def later_filter_kernel(rows, start_ref, across_ref, slice_ref, *outs):
    for angle in range(across_ref.shape[0]):
        filter_rows(slice_ref, start_ref, across_ref[angle], outs, angle, rows)


def tile_groups(count):
    group = next(g for g in (48, 32, 16, 8) if count % g == 0)
    return count // group, group


def start_tiles(tiles_ref, tile_scr, sems, groups, group):
    copies = []
    for g in range(groups):
        part = pl.ds(g * group, group)
        copies.append(pltpu.make_async_copy(tiles_ref.at[part], tile_scr.at[part], sems.at[g]))
    for copy in copies:
        copy.start()
    return copies


def tile_loop(live, copies, group, from_ref, to_ref, source, acc, tile_scr, dims):
    for g, copy in enumerate(copies):
        copy.wait()
        turns = jnp.clip((live - g * group + UNROLL - 1) // UNROLL, 0, group // UNROLL)

        def turn(i, carry):
            first = g * group + i * UNROLL
            found = [
                lax.dot_general(
                    source[from_ref[first + u]], tile_scr[first + u], (dims, ((), ())),
                    preferred_element_type=jnp.float32,
                )
                for u in range(UNROLL)
            ]
            for u in range(UNROLL):
                place = to_ref[first + u]
                acc[place] = acc[place] + found[u]
            return carry

        lax.fori_loop(0, turns, turn, 0)


def back_kernel(groups, group, live_ref, ray_ref, vox_ref, *refs):
    pieces = refs[: -7]
    tiles_ref, keep_out, send_out, ray_scr, tile_scr, acc, sems = refs[-7:]
    copies = start_tiles(tiles_ref, tile_scr, sems, groups, group)
    acc[...] = jnp.zeros_like(acc)
    held, _, columns = pieces[0].shape
    blocks = columns // LANES
    for m, piece in enumerate(pieces):
        for k in range(held):
            for b in range(blocks):
                ray_scr[(m * held + k) * blocks + b] = piece[k, :, b * LANES : (b + 1) * LANES]
    tile_loop(live_ref[0], copies, group, ray_ref, vox_ref, ray_scr, acc, tile_scr, ((1,), (0,)))
    half = keep_out.shape[0]
    keep_out[...] = acc[:half].astype(keep_out.dtype)
    send_out[...] = acc[half : 2 * half].astype(send_out.dtype)


def fore_kernel(groups, group, count, live_ref, vox_ref, ray_ref, *refs):
    pieces = refs[:count]
    tiles_ref = refs[count]
    outs = refs[count + 1 : -5]
    vox_scr, tile_scr, acc, sems, vox_sems = refs[-5:]
    vox_copies = []
    first = 0
    for i, piece in enumerate(pieces):
        size = piece.shape[0]
        vox_copies.append(pltpu.make_async_copy(piece, vox_scr.at[pl.ds(first, size)], vox_sems.at[i]))
        first += size
    for copy in vox_copies:
        copy.start()
    copies = start_tiles(tiles_ref, tile_scr, sems, groups, group)
    acc[...] = jnp.zeros_like(acc)
    for copy in vox_copies:
        copy.wait()
    tile_loop(live_ref[0], copies, group, vox_ref, ray_ref, vox_scr, acc, tile_scr, ((1,), (1,)))
    held, _, columns = outs[0].shape
    blocks = columns // LANES
    for m, out in enumerate(outs):
        for k in range(held):
            for b in range(blocks):
                out[k, :, b * LANES : (b + 1) * LANES] = acc[(m * held + k) * blocks + b].astype(out.dtype)


def update_kernel(kept_ref, came_ref, volume_ref, new_out, vox_out):
    for j in range(kept_ref.shape[0]):
        lanes = slice(j * LANES, (j + 1) * LANES)
        grad = kept_ref[j].astype(jnp.float32) + came_ref[j].astype(jnp.float32)
        new = jnp.clip(volume_ref[:, lanes] + step_size * grad, 0.0, 1.0)
        new_out[:, lanes] = new
        vox_out[j] = new.astype(vox_out.dtype)


def place_kernel(rows, count, start_ref, *refs):
    pieces = refs[:count]
    out, sems = refs[-2:]
    copies = [
        pltpu.make_async_copy(
            piece, out.at[:, pl.ds(pl.multiple_of(start_ref[m], rows), rows), :], sems.at[m]
        )
        for m, piece in enumerate(pieces)
    ]
    for copy in copies:
        copy.start()
    for copy in copies:
        copy.wait()


def add(a, b):
    return (a.astype(jnp.float32) + b.astype(jnp.float32)).astype(jnp.bfloat16)


def per_device(
    measured, predicted, slice_filter, column_filter, volume, tiles, tile_ray, tile_vox, live_tiles
):
    bf16, f32, i32 = jnp.bfloat16, jnp.float32, jnp.int32
    held, slices, columns = measured.shape
    angles, panels = lax.axis_size("angle"), lax.axis_size("panel")
    me_angle, me_panel = lax.axis_index("angle"), lax.axis_index("panel")
    rows_dev, vox_dev = volume.shape
    chunks = max(1, min(CHUNKS, rows_dev // 16))
    rows = rows_dev // chunks
    blocks = columns // LANES
    ray_dev = held * blocks
    ray_blocks = ray_dev * angles
    block_dev = vox_dev // LANES
    vox_blocks = block_dev * panels
    slots = tiles.shape[0]
    groups, group = tile_groups(slots)
    bits = [1 << b for b in range(panels.bit_length() - 1)]

    rel = (tile_vox // block_dev) ^ me_panel
    order = jnp.zeros_like(rel)
    for b in range(len(bits)):
        order = order | (((rel >> b) & 1) << (len(bits) - 1 - b))
    vox_place = order * block_dev + tile_vox % block_dev
    ray_place = ((tile_ray // ray_dev) ^ me_angle) * ray_dev + tile_ray % ray_dev
    dead = jnp.arange(slots, dtype=i32) >= live_tiles[0]
    vox_to = jnp.where(dead, vox_blocks, vox_place).astype(i32)
    ray_to = jnp.where(dead, ray_blocks, ray_place).astype(i32)

    partners = me_angle ^ jnp.arange(angles, dtype=i32)
    piece_shape = jax.ShapeDtypeStruct((held, rows, columns), bf16)

    def starts(c):
        return partners * rows_dev + c * rows

    def filtered(c, across):
        if c == 0:
            return pl.pallas_call(
                functools.partial(first_filter_kernel, rows),
                out_shape=(jax.ShapeDtypeStruct(measured.shape, bf16),) + (piece_shape,) * angles,
                in_specs=[SMEM_SPEC] + [VMEM_SPEC] * 4,
                out_specs=(VMEM_SPEC,) * (1 + angles),
                compiler_params=params(),
                name="first_filter",
            )(starts(c), measured, predicted, slice_filter, column_filter)
        return (across,) + tuple(
            pl.pallas_call(
                functools.partial(later_filter_kernel, rows),
                out_shape=(piece_shape,) * angles,
                in_specs=[SMEM_SPEC] + [VMEM_SPEC] * 2,
                out_specs=(VMEM_SPEC,) * angles,
                compiler_params=params(),
                name="later_filter",
            )(starts(c), across, slice_filter)
        )

    tile_scratch = pltpu.VMEM(tiles.shape, bf16)
    tile_sems = pltpu.SemaphoreType.DMA((groups,))

    def back(pieces):
        half = jax.ShapeDtypeStruct((vox_blocks // 2, rows, LANES), bf16)
        return pl.pallas_call(
            functools.partial(back_kernel, groups, group),
            out_shape=(half, half),
            in_specs=[SMEM_SPEC] * 3 + [VMEM_SPEC] * angles + [ANY_SPEC],
            out_specs=(VMEM_SPEC, VMEM_SPEC),
            scratch_shapes=[
                pltpu.VMEM((ray_blocks, rows, LANES), bf16),
                tile_scratch,
                pltpu.VMEM((vox_blocks + 1, rows, LANES), f32),
                tile_sems,
            ],
            compiler_params=params(),
            name="back",
        )(live_tiles, ray_place, vox_to, *pieces, tiles)

    def fore(pieces):
        return pl.pallas_call(
            functools.partial(fore_kernel, groups, group, len(pieces)),
            out_shape=(piece_shape,) * angles,
            in_specs=[SMEM_SPEC] * 3 + [ANY_SPEC] * (len(pieces) + 1),
            out_specs=(VMEM_SPEC,) * angles,
            scratch_shapes=[
                pltpu.VMEM((vox_blocks, rows, LANES), bf16),
                tile_scratch,
                pltpu.VMEM((ray_blocks + 1, rows, LANES), f32),
                tile_sems,
                pltpu.SemaphoreType.DMA((len(pieces),)),
            ],
            compiler_params=params(),
            name="fore",
        )(live_tiles, vox_place, ray_to, *pieces, tiles)

    def update(c, kept, came):
        whole = pl.BlockSpec((block_dev, rows, LANES), lambda i: (0, 0, 0))
        return pl.pallas_call(
            update_kernel,
            grid=(1,),
            out_shape=(
                jax.ShapeDtypeStruct((rows, vox_dev), f32),
                jax.ShapeDtypeStruct((block_dev, rows, LANES), bf16),
            ),
            in_specs=[whole, whole, pl.BlockSpec((rows, vox_dev), lambda i, c=c: (c, 0))],
            out_specs=(pl.BlockSpec((rows, vox_dev), lambda i: (0, 0)), whole),
            compiler_params=params(),
            name="update",
        )(kept, came, volume)

    def place(c, pieces, out):
        extra = () if out is None else (out,)
        return pl.pallas_call(
            functools.partial(place_kernel, rows, angles),
            out_shape=jax.ShapeDtypeStruct(measured.shape, bf16),
            in_specs=[SMEM_SPEC] + [VMEM_SPEC] * angles + [ANY_SPEC] * len(extra),
            out_specs=ANY_SPEC,
            scratch_shapes=[pltpu.SemaphoreType.DMA((angles,))],
            input_output_aliases={1 + angles: 0} if extra else {},
            compiler_params=params(),
            name="place",
        )(starts(c), *pieces, *extra)

    across = None
    rays = []
    for c in range(chunks):
        across, *pieces = filtered(c, across)
        rays.append([pieces[0]] + [swap(pieces[m], "angle", m) for m in range(1, angles)])

    new_parts, projected = [], []
    for c in range(chunks):
        kept, sent = back(rays[c])
        for bit in bits[:-1]:
            came = swap(sent, "panel", bit)
            half = kept.shape[0] // 2
            kept, sent = add(kept[:half], came[:half]), add(kept[half:], came[half:])
        came = swap(sent, "panel", bits[-1])
        new_part, vox = update(c, kept, came)
        new_parts.append(new_part)
        parts = [vox]
        for bit in bits[::-1]:
            parts = parts + [swap(part, "panel", bit) for part in parts]
        outs = fore(parts)
        projected.append([outs[0]] + [swap(outs[m], "angle", m) for m in range(1, angles)])

    out = None
    for c in range(chunks):
        out = place(c, projected[c], out)
    return (jnp.concatenate(new_parts, axis=0), out)


def solution(mesh):
    in_specs = (
        P(("angle", "panel"), None, None),
        P(("angle", "panel"), None, None),
        P(),
        P(),
        P("angle", "panel"),
        P("panel", None, None),
        P("panel"),
        P("panel"),
        P("panel"),
    )
    out_specs = (P("angle", "panel"), P(("angle", "panel"), None, None))
    return jax.shard_map(
        per_device, mesh=mesh, in_specs=in_specs, out_specs=out_specs, check_vma=False
    )
```

```python
import functools

import jax
import jax.numpy as jnp
from jax import lax
from jax.experimental import pallas as pl
from jax.experimental.pallas import tpu as pltpu
from jax.sharding import PartitionSpec as P


step_size = 0.1
LANES = 128
UNROLL = 48
AHEAD = 4
FILTER_STEPS = 2
CUTS = (1, 1)
MIB = 1024 * 1024


VMEM_SPEC = pl.BlockSpec(memory_space=pltpu.VMEM)
ANY_SPEC = pl.BlockSpec(memory_space=pl.ANY)
HBM_SPEC = pl.BlockSpec(memory_space=pltpu.HBM)
SMEM_SPEC = pl.BlockSpec(memory_space=pltpu.SMEM)


def params(mib):
    return pltpu.CompilerParams(vmem_limit_bytes=mib * MIB)


def row_parts(rows_dev):
    cuts = CUTS
    while len(cuts) > 1 and rows_dev * min(cuts) < 16 * sum(cuts):
        cuts = (1,) * (len(cuts) - 1)
    return [rows_dev * cut // sum(cuts) for cut in cuts]


def swap_bits(panels):
    return [1 << b for b in range(panels.bit_length() - 1)]


def swap_mask(index, step, bits):
    far = bits[1:]
    return far[step] if index % 2 == 0 else far[len(far) - 1 - step]


def swap_far(value, step, bits):
    size = lax.axis_size("panel")
    return lax.ppermute(value, "panel", [(i, i ^ swap_mask(i, step, bits)) for i in range(size)])


def cost(us):
    return pl.CostEstimate(flops=int(us * 1e9), bytes_accessed=0, transcendentals=0)


def swap(value, axis, mask):
    size = lax.axis_size(axis)
    return lax.ppermute(value, axis, [(i, i ^ mask) for i in range(size)])


def filter_rows(slice_ref, start_of, across, outs, angle, rows):
    picked = jnp.concatenate(
        [slice_ref[pl.ds(pl.multiple_of(start_of(m), 16), rows), :] for m in range(len(outs))], axis=0
    )
    result = jnp.dot(picked, across, preferred_element_type=jnp.float32).astype(jnp.bfloat16)
    for m, out in enumerate(outs):
        out[angle] = result[m * rows : (m + 1) * rows]


def first_filter_kernel(rows, start_of, measured, predicted, slice_ref, column_ref, across_out, *refs):
    outs = refs[:-5]
    measured_scr, predicted_scr, slice_scr, column_scr, sems = refs[-5:]
    held, slices, _ = measured.shape
    step = slices // FILTER_STEPS
    places = [(angle, pl.ds(i * step, step)) for angle in range(held) for i in range(FILTER_STEPS)]
    pairs = [
        [
            pltpu.make_async_copy(predicted.at[place], predicted_scr.at[place], sems.at[2 * i]),
            pltpu.make_async_copy(measured.at[place], measured_scr.at[place], sems.at[2 * i + 1]),
        ]
        for i, place in enumerate(places)
    ]
    column_copy = pltpu.make_async_copy(column_ref, column_scr, sems.at[2 * len(places)])
    slice_copy = pltpu.make_async_copy(slice_ref, slice_scr, sems.at[2 * len(places) + 1])
    for copy in pairs[0] + [column_copy]:
        copy.start()
    for i, (angle, part) in enumerate(places):
        for copy in pairs[i]:
            copy.wait()
        if i == 0:
            for copy in sum(pairs[1:], []) + [slice_copy]:
                copy.start()
        bright = jnp.exp(-predicted_scr[angle, part].astype(jnp.float32))
        misfit = ((measured_scr[angle, part].astype(jnp.float32) - bright) * bright).astype(jnp.bfloat16)
        if i == 0:
            column_copy.wait()
        across = jnp.dot(misfit, column_scr[...], preferred_element_type=jnp.float32)
        across_out[angle, part] = across.astype(jnp.bfloat16)
        if i % FILTER_STEPS == FILTER_STEPS - 1:
            if angle == 0:
                slice_copy.wait()
            filter_rows(slice_scr, start_of, across_out[angle], outs, angle, rows)


def later_filter_kernel(rows, start_of, across_ref, slice_ref, *outs):
    for angle in range(across_ref.shape[0]):
        filter_rows(slice_ref, start_of, across_ref[angle], outs, angle, rows)


def tile_groups(count):
    group = next(g for g in (48, 32, 16, 8) if count % g == 0)
    return count // group, group


def start_tiles(tiles_ref, tile_scr, sems):
    count = tiles_ref.shape[0]
    groups, group = tile_groups(count)
    copies = []
    for g in range(groups):
        part = pl.ds(g * group, group)
        copies.append(pltpu.make_async_copy(tiles_ref.at[part], tile_scr.at[part], sems.at[g]))
    for copy in copies[:AHEAD]:
        copy.start()
    return copies


def tile_loop(live, copies, from_ref, to_ref, source, tiles, accs, held, dims):
    turns = (live + UNROLL - 1) // UNROLL

    def multiply(first):
        for u in range(UNROLL):
            held[u] = lax.dot_general(
                source[from_ref[first + u]], tiles[first + u], (dims, ((), ())),
                preferred_element_type=jnp.float32,
            )

    def accumulate(first):
        for u in range(UNROLL):
            place, into = to_ref[first + u], accs[u % len(accs)]
            into[place] = into[place] + held[u]

    def turn(i, carry):
        accumulate((i - 1) * UNROLL)
        multiply(i * UNROLL)
        return carry

    if copies is None:
        multiply(0)
        lax.fori_loop(1, turns, turn, 0)
    else:
        each = tiles.shape[0] // len(copies) // UNROLL
        for g, copy in enumerate(copies):
            copy.wait()
            if g + AHEAD < len(copies):
                copies[g + AHEAD].start()
            if g == 0:
                multiply(0)
            lax.fori_loop(max(1, g * each), jnp.minimum(turns, (g + 1) * each), turn, 0)
    accumulate((turns - 1) * UNROLL)


def back_kernel(live_ref, ray_ref, vox_ref, *refs):
    pieces = refs[:-9]
    tiles_ref, keep_out, send_out, ray_scr, tile_scr, acc, more, products, sems = refs[-9:]
    copies = start_tiles(tiles_ref, tile_scr, sems)
    acc[...] = jnp.zeros_like(acc)
    more[...] = jnp.zeros_like(more)
    held, _, columns = pieces[0].shape
    blocks = columns // LANES
    for m, piece in enumerate(pieces):
        for k in range(held):
            for b in range(blocks):
                ray_scr[(m * held + k) * blocks + b] = piece[k, :, b * LANES : (b + 1) * LANES]
    tile_loop(live_ref[0], copies, ray_ref, vox_ref, ray_scr, tile_scr, (acc, more), products, ((1,), (0,)))
    half = keep_out.shape[0]
    for i in range(half):
        keep_out[i] = (acc[i] + more[i]).astype(keep_out.dtype)
        send_out[i] = (acc[half + i] + more[half + i]).astype(send_out.dtype)


def fore_kernel(count, live_ref, vox_ref, ray_ref, *refs):
    pieces = refs[:count]
    tiles_ref = refs[count]
    outs = refs[count + 1 : -5]
    vox_scr, acc, more, products, vox_sems = refs[-5:]
    vox_copies = []
    first = 0
    for i, piece in enumerate(pieces):
        size = piece.shape[0]
        vox_copies.append(pltpu.make_async_copy(piece, vox_scr.at[pl.ds(first, size)], vox_sems.at[i]))
        first += size
    for copy in vox_copies:
        copy.start()
    acc[...] = jnp.zeros_like(acc)
    more[...] = jnp.zeros_like(more)
    for copy in vox_copies:
        copy.wait()
    tile_loop(live_ref[0], None, vox_ref, ray_ref, vox_scr, tiles_ref, (acc, more), products, ((1,), (1,)))
    held, _, columns = outs[0].shape
    blocks = columns // LANES
    for m, out in enumerate(outs):
        for k in range(held):
            for b in range(blocks):
                block = (m * held + k) * blocks + b
                out[k, :, b * LANES : (b + 1) * LANES] = (acc[block] + more[block]).astype(out.dtype)


def update_kernel(first, kept_ref, came_ref, volume_ref, new_out, vox_out):
    for j in range(kept_ref.shape[0]):
        lanes = slice(j * LANES, (j + 1) * LANES)
        grad = kept_ref[j].astype(jnp.float32) + came_ref[j].astype(jnp.float32)
        new = jnp.clip(volume_ref[first : first + kept_ref.shape[1], lanes] + step_size * grad, 0.0, 1.0)
        new_out[:, lanes] = new
        vox_out[j] = new.astype(vox_out.dtype)


def place_kernel(rows, count, start_of, *refs):
    pieces = refs[:count]
    out, sems = refs[-2:]
    copies = [
        pltpu.make_async_copy(
            piece, out.at[:, pl.ds(pl.multiple_of(start_of(m), 16), rows), :], sems.at[m]
        )
        for m, piece in enumerate(pieces)
    ]
    for copy in copies:
        copy.start()
    for copy in copies:
        copy.wait()


def add(a, b):
    return (a.astype(jnp.float32) + b.astype(jnp.float32)).astype(jnp.bfloat16)


def per_device(
    measured, predicted, slice_filter, column_filter, volume, tiles, tile_ray, tile_vox, live_tiles
):
    far_tiles = pltpu.with_memory_space_constraint(tiles, pltpu.HBM)
    bf16, f32, i32 = jnp.bfloat16, jnp.float32, jnp.int32
    held, _, columns = measured.shape
    angles, panels = lax.axis_size("angle"), lax.axis_size("panel")
    me_angle, me_panel = lax.axis_index("angle"), lax.axis_index("panel")
    rows_dev, vox_dev = volume.shape
    parts_rows = row_parts(rows_dev)
    offsets = [sum(parts_rows[:c]) for c in range(len(parts_rows))]
    chunks = len(parts_rows)
    blocks = columns // LANES
    ray_dev = held * blocks
    ray_blocks = ray_dev * angles
    block_dev = vox_dev // LANES
    vox_blocks = block_dev * panels
    slots = tiles.shape[0]
    bits = swap_bits(panels)

    rel = (tile_vox // block_dev) ^ me_panel
    order = (rel & 1) << (len(bits) - 1)
    for step in range(len(bits) - 1):
        mask = jnp.where((tile_vox // block_dev) % 2 == 0, swap_mask(0, step, bits), swap_mask(1, step, bits))
        order = order | (jnp.where((rel & mask) != 0, 1, 0) << (len(bits) - 2 - step))
    vox_place = order * block_dev + tile_vox % block_dev
    ray_place = ((tile_ray // ray_dev) ^ me_angle) * ray_dev + tile_ray % ray_dev
    dead = jnp.arange(slots, dtype=i32) >= live_tiles[0]
    vox_to = jnp.where(dead, vox_blocks, vox_place).astype(i32)
    ray_to = jnp.where(dead, ray_blocks, ray_place).astype(i32)


    def piece_shape(c):
        return jax.ShapeDtypeStruct((held, parts_rows[c], columns), bf16)

    def starts(c):
        return lambda m: (lax.axis_index("angle") ^ m) * rows_dev + offsets[c]

    def filtered(c, across):
        rows = parts_rows[c]
        if c == 0:
            return pl.pallas_call(
                functools.partial(first_filter_kernel, rows, starts(c)),
                out_shape=(jax.ShapeDtypeStruct(measured.shape, bf16),) + (piece_shape(c),) * angles,
                in_specs=[HBM_SPEC] * 4,
                out_specs=(VMEM_SPEC,) * (1 + angles),
                scratch_shapes=[
                    pltpu.VMEM(measured.shape, bf16),
                    pltpu.VMEM(predicted.shape, bf16),
                    pltpu.VMEM(slice_filter.shape, bf16),
                    pltpu.VMEM(column_filter.shape, bf16),
                    pltpu.SemaphoreType.DMA((2 * held * FILTER_STEPS + 2,)),
                ],
                compiler_params=params(58),
                cost_estimate=cost(7),
                name="first_filter",
            )(measured, predicted, slice_filter, column_filter)
        return (across,) + tuple(
            pl.pallas_call(
                functools.partial(later_filter_kernel, rows, starts(c)),
                out_shape=(piece_shape(c),) * angles,
                in_specs=[VMEM_SPEC] * 2,
                out_specs=(VMEM_SPEC,) * angles,
                compiler_params=params(20),
                cost_estimate=cost(2),
                name="later_filter",
            )(across, slice_filter)
        )

    tile_scratch = pltpu.VMEM(tiles.shape, bf16)
    tile_sems = pltpu.SemaphoreType.DMA((tile_groups(slots)[0],))

    def back(c, pieces):
        rows = parts_rows[c]
        half = jax.ShapeDtypeStruct((vox_blocks // 2, rows, LANES), bf16)
        return pl.pallas_call(
            back_kernel,
            out_shape=(half, half),
            in_specs=[SMEM_SPEC] * 3 + [VMEM_SPEC] * angles + [HBM_SPEC],
            out_specs=(VMEM_SPEC, VMEM_SPEC),
            scratch_shapes=[
                pltpu.VMEM((ray_blocks, rows, LANES), bf16),
                tile_scratch,
                pltpu.VMEM((vox_blocks + 1, rows, LANES), f32),
                pltpu.VMEM((vox_blocks + 1, rows, LANES), f32),
                pltpu.VMEM((UNROLL, rows, LANES), f32),
                tile_sems,
            ],
            compiler_params=params(26),
            cost_estimate=cost(6),
            name="back",
        )(live_tiles, ray_place, vox_to, *pieces, far_tiles)

    def fore(c, pieces):
        rows = parts_rows[c]
        return pl.pallas_call(
            functools.partial(fore_kernel, len(pieces)),
            out_shape=(piece_shape(c),) * angles,
            in_specs=[SMEM_SPEC] * 3 + [ANY_SPEC] * len(pieces) + [VMEM_SPEC],
            out_specs=(VMEM_SPEC,) * angles,
            scratch_shapes=[
                pltpu.VMEM((vox_blocks, rows, LANES), bf16),
                pltpu.VMEM((ray_blocks + 1, rows, LANES), f32),
                pltpu.VMEM((ray_blocks + 1, rows, LANES), f32),
                pltpu.VMEM((UNROLL, rows, LANES), f32),
                pltpu.SemaphoreType.DMA((len(pieces),)),
            ],
            compiler_params=params(26),
            cost_estimate=cost(8),
            name="fore",
        )(live_tiles, vox_place, ray_to, *pieces, tiles)

    def update(c, kept, came):
        rows = parts_rows[c]
        return pl.pallas_call(
            functools.partial(update_kernel, offsets[c]),
            out_shape=(
                jax.ShapeDtypeStruct((rows, vox_dev), f32),
                jax.ShapeDtypeStruct((block_dev, rows, LANES), bf16),
            ),
            in_specs=[VMEM_SPEC] * 3,
            out_specs=(VMEM_SPEC, VMEM_SPEC),
            compiler_params=params(20),
            cost_estimate=cost(1),
            name="update",
        )(kept, came, volume)

    def place(c, pieces, out):
        extra = () if out is None else (out,)
        return pl.pallas_call(
            functools.partial(place_kernel, parts_rows[c], angles, starts(c)),
            out_shape=jax.ShapeDtypeStruct(measured.shape, bf16),
            in_specs=[VMEM_SPEC] * angles + [ANY_SPEC] * len(extra),
            out_specs=ANY_SPEC,
            scratch_shapes=[pltpu.SemaphoreType.DMA((angles,))],
            input_output_aliases={angles: 0} if extra else {},
            compiler_params=params(20),
            cost_estimate=cost(1),
            name="place",
        )(*pieces, *extra)

    def spread(pieces):
        came = [pieces[0]]
        for m in range(1, angles):
            came.append(swap(pieces[m], "angle", m))
        return came

    across = None
    rays, new_parts, projected = [], [], []
    for c in range(chunks):
        across, *pieces = filtered(c, across)
        rays.append(spread(pieces))
    for c in range(chunks):
        kept, sent = back(c, rays[c])
        came = swap(sent, "panel", 1)
        half = kept.shape[0] // 2
        sent, kept = add(kept[half:], came[half:]), add(kept[:half], came[:half])
        for step in range(len(bits) - 1):
            came = swap_far(sent, step, bits)
            if step < len(bits) - 2:
                half = kept.shape[0] // 2
                sent, kept = add(kept[half:], came[half:]), add(kept[:half], came[:half])
        new_part, parts = update(c, kept, came)
        new_parts.append(new_part)
        for step in range(len(bits) - 2, -1, -1):
            came = swap_far(parts, step, bits)
            if step:
                parts = jnp.concatenate([parts, came], axis=0)
        pieces = [parts, came]
        for i in range(2):
            pieces.append(swap(pieces[i], "panel", 1))
        outs = fore(c, pieces)
        projected.append(spread(outs))
    out = None
    for c in range(chunks):
        out = place(c, projected[c], out)
    return (jnp.concatenate(new_parts, axis=0), out)


def solution(mesh):
    in_specs = (
        P(("angle", "panel"), None, None),
        P(("angle", "panel"), None, None),
        P(),
        P(),
        P("angle", "panel"),
        P("panel", None, None),
        P("panel"),
        P("panel"),
        P("panel"),
    )
    out_specs = (P("angle", "panel"), P(("angle", "panel"), None, None))
    return jax.shard_map(
        per_device, mesh=mesh, in_specs=in_specs, out_specs=out_specs, check_vma=False
    )
```

```python
import functools

import jax
import jax.numpy as jnp
from jax import lax
from jax.experimental import pallas as pl
from jax.experimental.pallas import tpu as pltpu
from jax.sharding import PartitionSpec as P


step_size = 0.1
LANES = 128
UNROLL = 48
AHEAD = 4
FILTER_STEPS = 2
CUTS = (2, 4, 2)
MIB = 1024 * 1024


VMEM_SPEC = pl.BlockSpec(memory_space=pltpu.VMEM)
ANY_SPEC = pl.BlockSpec(memory_space=pl.ANY)
HBM_SPEC = pl.BlockSpec(memory_space=pltpu.HBM)
SMEM_SPEC = pl.BlockSpec(memory_space=pltpu.SMEM)


def params(mib):
    return pltpu.CompilerParams(vmem_limit_bytes=mib * MIB)


def row_parts(rows_dev):
    cuts = CUTS
    while len(cuts) > 1 and rows_dev * min(cuts) < 16 * sum(cuts):
        cuts = (1,) * (len(cuts) - 1)
    return [rows_dev * cut // sum(cuts) for cut in cuts]


def swap_bits(panels):
    return [1 << b for b in range(panels.bit_length() - 1)]


def swap_mask(index, step, bits):
    far = bits[1:]
    return far[step] if index % 2 == 0 else far[len(far) - 1 - step]


def swap_far(value, step, bits):
    size = lax.axis_size("panel")
    return lax.ppermute(value, "panel", [(i, i ^ swap_mask(i, step, bits)) for i in range(size)])


def cost(us):
    return pl.CostEstimate(flops=int(us * 1e9), bytes_accessed=0, transcendentals=0)


def swap(value, axis, mask):
    size = lax.axis_size(axis)
    return lax.ppermute(value, axis, [(i, i ^ mask) for i in range(size)])


def filter_rows(slice_ref, start_of, across, outs, angle, rows):
    picked = jnp.concatenate(
        [slice_ref[pl.ds(pl.multiple_of(start_of(m), 16), rows), :] for m in range(len(outs))], axis=0
    )
    result = jnp.dot(picked, across, preferred_element_type=jnp.float32).astype(jnp.bfloat16)
    for m, out in enumerate(outs):
        out[angle] = result[m * rows : (m + 1) * rows]


def first_filter_kernel(rows, start_of, measured, predicted, slice_ref, column_ref, across_out, *refs):
    outs = refs[:-5]
    measured_scr, predicted_scr, slice_scr, column_scr, sems = refs[-5:]
    held, slices, _ = measured.shape
    step = slices // FILTER_STEPS
    places = [(angle, pl.ds(i * step, step)) for angle in range(held) for i in range(FILTER_STEPS)]
    pairs = [
        [
            pltpu.make_async_copy(predicted.at[place], predicted_scr.at[place], sems.at[2 * i]),
            pltpu.make_async_copy(measured.at[place], measured_scr.at[place], sems.at[2 * i + 1]),
        ]
        for i, place in enumerate(places)
    ]
    column_copy = pltpu.make_async_copy(column_ref, column_scr, sems.at[2 * len(places)])
    slice_copy = pltpu.make_async_copy(slice_ref, slice_scr, sems.at[2 * len(places) + 1])
    for copy in pairs[0] + [column_copy]:
        copy.start()
    for i, (angle, part) in enumerate(places):
        for copy in pairs[i]:
            copy.wait()
        if i == 0:
            for copy in sum(pairs[1:], []) + [slice_copy]:
                copy.start()
        bright = jnp.exp(-predicted_scr[angle, part].astype(jnp.float32))
        misfit = ((measured_scr[angle, part].astype(jnp.float32) - bright) * bright).astype(jnp.bfloat16)
        if i == 0:
            column_copy.wait()
        across = jnp.dot(misfit, column_scr[...], preferred_element_type=jnp.float32)
        across_out[angle, part] = across.astype(jnp.bfloat16)
        if i % FILTER_STEPS == FILTER_STEPS - 1:
            if angle == 0:
                slice_copy.wait()
            filter_rows(slice_scr, start_of, across_out[angle], outs, angle, rows)


def later_filter_kernel(rows, starts, across_ref, slice_ref, *outs):
    each = len(outs) // len(rows)
    for c in range(len(rows)):
        for angle in range(across_ref.shape[0]):
            filter_rows(slice_ref, starts[c], across_ref[angle], outs[c * each : (c + 1) * each], angle, rows[c])


def tile_groups(count):
    group = next(g for g in (48, 32, 16, 8) if count % g == 0)
    return count // group, group


def start_tiles(tiles_ref, tile_scr, sems):
    count = tiles_ref.shape[0]
    groups, group = tile_groups(count)
    copies = []
    for g in range(groups):
        part = pl.ds(g * group, group)
        copies.append(pltpu.make_async_copy(tiles_ref.at[part], tile_scr.at[part], sems.at[g]))
    for copy in copies[:AHEAD]:
        copy.start()
    return copies


def tile_loop(live, copies, from_ref, to_ref, source, tiles, accs, held, dims):
    turns = (live + UNROLL - 1) // UNROLL

    def multiply(first):
        for u in range(UNROLL):
            held[u] = lax.dot_general(
                source[from_ref[first + u]], tiles[first + u], (dims, ((), ())),
                preferred_element_type=jnp.float32,
            )

    def accumulate(first):
        for u in range(UNROLL):
            place, into = to_ref[first + u], accs[u % len(accs)]
            into[place] = into[place] + held[u]

    def turn(i, carry):
        accumulate((i - 1) * UNROLL)
        multiply(i * UNROLL)
        return carry

    if copies is None:
        multiply(0)
        lax.fori_loop(1, turns, turn, 0)
    else:
        each = tiles.shape[0] // len(copies) // UNROLL
        for g, copy in enumerate(copies):
            copy.wait()
            if g + AHEAD < len(copies):
                copies[g + AHEAD].start()
            if g == 0:
                multiply(0)
            lax.fori_loop(max(1, g * each), jnp.minimum(turns, (g + 1) * each), turn, 0)
    accumulate((turns - 1) * UNROLL)


def back_kernel(live_ref, ray_ref, vox_ref, *refs):
    pieces = refs[:-9]
    tiles_ref, keep_out, send_out, ray_scr, tile_scr, acc, more, products, sems = refs[-9:]
    copies = start_tiles(tiles_ref, tile_scr, sems)
    acc[...] = jnp.zeros_like(acc)
    more[...] = jnp.zeros_like(more)
    held, _, columns = pieces[0].shape
    blocks = columns // LANES
    for m, piece in enumerate(pieces):
        for k in range(held):
            for b in range(blocks):
                ray_scr[(m * held + k) * blocks + b] = piece[k, :, b * LANES : (b + 1) * LANES]
    tile_loop(live_ref[0], copies, ray_ref, vox_ref, ray_scr, tile_scr, (acc, more), products, ((1,), (0,)))
    half = keep_out.shape[0]
    for i in range(half):
        keep_out[i] = (acc[i] + more[i]).astype(keep_out.dtype)
        send_out[i] = (acc[half + i] + more[half + i]).astype(send_out.dtype)


def fore_kernel(count, live_ref, vox_ref, ray_ref, *refs):
    pieces = refs[:count]
    tiles_ref = refs[count]
    outs = refs[count + 1 : -5]
    vox_scr, acc, more, products, vox_sems = refs[-5:]
    vox_copies = []
    first = 0
    for i, piece in enumerate(pieces):
        size = piece.shape[0]
        vox_copies.append(pltpu.make_async_copy(piece, vox_scr.at[pl.ds(first, size)], vox_sems.at[i]))
        first += size
    for copy in vox_copies:
        copy.start()
    acc[...] = jnp.zeros_like(acc)
    more[...] = jnp.zeros_like(more)
    for copy in vox_copies:
        copy.wait()
    tile_loop(live_ref[0], None, vox_ref, ray_ref, vox_scr, tiles_ref, (acc, more), products, ((1,), (1,)))
    held, _, columns = outs[0].shape
    blocks = columns // LANES
    for m, out in enumerate(outs):
        for k in range(held):
            for b in range(blocks):
                block = (m * held + k) * blocks + b
                out[k, :, b * LANES : (b + 1) * LANES] = (acc[block] + more[block]).astype(out.dtype)


def update_kernel(first, kept_ref, came_ref, volume_ref, new_out, vox_out):
    for j in range(kept_ref.shape[0]):
        lanes = slice(j * LANES, (j + 1) * LANES)
        grad = kept_ref[j].astype(jnp.float32) + came_ref[j].astype(jnp.float32)
        new = jnp.clip(volume_ref[first : first + kept_ref.shape[1], lanes] + step_size * grad, 0.0, 1.0)
        new_out[:, lanes] = new
        vox_out[j] = new.astype(vox_out.dtype)


def place_kernel(rows, count, start_of, *refs):
    pieces = refs[:count]
    out, sems = refs[-2:]
    copies = [
        pltpu.make_async_copy(
            piece, out.at[:, pl.ds(pl.multiple_of(start_of(m), 16), rows), :], sems.at[m]
        )
        for m, piece in enumerate(pieces)
    ]
    for copy in copies:
        copy.start()
    for copy in copies:
        copy.wait()


def add(a, b):
    return (a.astype(jnp.float32) + b.astype(jnp.float32)).astype(jnp.bfloat16)


def per_device(
    measured, predicted, slice_filter, column_filter, volume, tiles, tile_ray, tile_vox, live_tiles
):
    far_tiles = pltpu.with_memory_space_constraint(tiles, pltpu.HBM)
    bf16, f32, i32 = jnp.bfloat16, jnp.float32, jnp.int32
    held, _, columns = measured.shape
    angles, panels = lax.axis_size("angle"), lax.axis_size("panel")
    me_angle, me_panel = lax.axis_index("angle"), lax.axis_index("panel")
    rows_dev, vox_dev = volume.shape
    parts_rows = row_parts(rows_dev)
    offsets = [sum(parts_rows[:c]) for c in range(len(parts_rows))]
    chunks = len(parts_rows)
    blocks = columns // LANES
    ray_dev = held * blocks
    ray_blocks = ray_dev * angles
    block_dev = vox_dev // LANES
    vox_blocks = block_dev * panels
    slots = tiles.shape[0]
    bits = swap_bits(panels)

    rel = (tile_vox // block_dev) ^ me_panel
    order = (rel & 1) << (len(bits) - 1)
    for step in range(len(bits) - 1):
        mask = jnp.where((tile_vox // block_dev) % 2 == 0, swap_mask(0, step, bits), swap_mask(1, step, bits))
        order = order | (jnp.where((rel & mask) != 0, 1, 0) << (len(bits) - 2 - step))
    vox_place = order * block_dev + tile_vox % block_dev
    ray_place = ((tile_ray // ray_dev) ^ me_angle) * ray_dev + tile_ray % ray_dev
    dead = jnp.arange(slots, dtype=i32) >= live_tiles[0]
    vox_to = jnp.where(dead, vox_blocks, vox_place).astype(i32)
    ray_to = jnp.where(dead, ray_blocks, ray_place).astype(i32)


    def piece_shape(c):
        return jax.ShapeDtypeStruct((held, parts_rows[c], columns), bf16)

    def starts(c):
        return lambda m: (lax.axis_index("angle") ^ m) * rows_dev + offsets[c]

    def first_filtered():
        return pl.pallas_call(
            functools.partial(first_filter_kernel, parts_rows[0], starts(0)),
            out_shape=(jax.ShapeDtypeStruct(measured.shape, bf16),) + (piece_shape(0),) * angles,
            in_specs=[HBM_SPEC] * 4,
            out_specs=(VMEM_SPEC,) * (1 + angles),
            scratch_shapes=[
                pltpu.VMEM(measured.shape, bf16),
                pltpu.VMEM(predicted.shape, bf16),
                pltpu.VMEM(slice_filter.shape, bf16),
                pltpu.VMEM(column_filter.shape, bf16),
                pltpu.SemaphoreType.DMA((2 * held * FILTER_STEPS + 2,)),
            ],
            compiler_params=params(58),
            cost_estimate=cost(7),
            name="first_filter",
        )(measured, predicted, slice_filter, column_filter)

    def later_filtered(across):
        later = range(1, chunks)
        outs = pl.pallas_call(
            functools.partial(later_filter_kernel, parts_rows[1:], [starts(c) for c in later]),
            out_shape=tuple(piece_shape(c) for c in later for _ in range(angles)),
            in_specs=[VMEM_SPEC] * 2,
            out_specs=(VMEM_SPEC,) * (len(later) * angles),
            compiler_params=params(20),
            cost_estimate=cost(2),
            name="later_filter",
        )(across, slice_filter)
        return [outs[c * angles : (c + 1) * angles] for c in range(len(later))]

    tile_scratch = pltpu.VMEM(tiles.shape, bf16)
    tile_sems = pltpu.SemaphoreType.DMA((tile_groups(slots)[0],))

    def back(c, pieces):
        rows = parts_rows[c]
        half = jax.ShapeDtypeStruct((vox_blocks // 2, rows, LANES), bf16)
        return pl.pallas_call(
            back_kernel,
            out_shape=(half, half),
            in_specs=[SMEM_SPEC] * 3 + [VMEM_SPEC] * angles + [HBM_SPEC],
            out_specs=(VMEM_SPEC, VMEM_SPEC),
            scratch_shapes=[
                pltpu.VMEM((ray_blocks, rows, LANES), bf16),
                tile_scratch,
                pltpu.VMEM((vox_blocks + 1, rows, LANES), f32),
                pltpu.VMEM((vox_blocks + 1, rows, LANES), f32),
                pltpu.VMEM((UNROLL, rows, LANES), f32),
                tile_sems,
            ],
            compiler_params=params(26),
            cost_estimate=cost(6),
            name="back",
        )(live_tiles, ray_place, vox_to, *pieces, far_tiles)

    def fore(c, pieces):
        rows = parts_rows[c]
        return pl.pallas_call(
            functools.partial(fore_kernel, len(pieces)),
            out_shape=(piece_shape(c),) * angles,
            in_specs=[SMEM_SPEC] * 3 + [ANY_SPEC] * len(pieces) + [VMEM_SPEC],
            out_specs=(VMEM_SPEC,) * angles,
            scratch_shapes=[
                pltpu.VMEM((vox_blocks, rows, LANES), bf16),
                pltpu.VMEM((ray_blocks + 1, rows, LANES), f32),
                pltpu.VMEM((ray_blocks + 1, rows, LANES), f32),
                pltpu.VMEM((UNROLL, rows, LANES), f32),
                pltpu.SemaphoreType.DMA((len(pieces),)),
            ],
            compiler_params=params(26),
            cost_estimate=cost(8),
            name="fore",
        )(live_tiles, vox_place, ray_to, *pieces, tiles)

    def update(c, kept, came):
        rows = parts_rows[c]
        return pl.pallas_call(
            functools.partial(update_kernel, offsets[c]),
            out_shape=(
                jax.ShapeDtypeStruct((rows, vox_dev), f32),
                jax.ShapeDtypeStruct((block_dev, rows, LANES), bf16),
            ),
            in_specs=[VMEM_SPEC] * 3,
            out_specs=(VMEM_SPEC, VMEM_SPEC),
            compiler_params=params(20),
            cost_estimate=cost(1),
            name="update",
        )(kept, came, volume)

    def place(c, pieces, out):
        extra = () if out is None else (out,)
        return pl.pallas_call(
            functools.partial(place_kernel, parts_rows[c], angles, starts(c)),
            out_shape=jax.ShapeDtypeStruct(measured.shape, bf16),
            in_specs=[VMEM_SPEC] * angles + [ANY_SPEC] * len(extra),
            out_specs=ANY_SPEC,
            scratch_shapes=[pltpu.SemaphoreType.DMA((angles,))],
            input_output_aliases={angles: 0} if extra else {},
            compiler_params=params(20),
            cost_estimate=cost(1),
            name="place",
        )(*pieces, *extra)

    def spread(pieces):
        came = [pieces[0]]
        for m in range(1, angles):
            came.append(swap(pieces[m], "angle", m))
        return came

    new_parts, projected = [], []
    across, *pieces = first_filtered()
    rays = [spread(pieces)]
    if chunks > 1:
        later = later_filtered(across)
        rays += [spread(later[c - 1]) for c in range(1, chunks)]
    for c in range(chunks):
        kept, sent = back(c, rays[c])
        came = swap(sent, "panel", 1)
        half = kept.shape[0] // 2
        sent, kept = add(kept[half:], came[half:]), add(kept[:half], came[:half])
        for step in range(len(bits) - 1):
            came = swap_far(sent, step, bits)
            if step < len(bits) - 2:
                half = kept.shape[0] // 2
                sent, kept = add(kept[half:], came[half:]), add(kept[:half], came[:half])
        new_part, parts = update(c, kept, came)
        new_parts.append(new_part)
        for step in range(len(bits) - 2, -1, -1):
            came = swap_far(parts, step, bits)
            if step:
                parts = jnp.concatenate([parts, came], axis=0)
        pieces = [parts, came]
        for i in range(2):
            pieces.append(swap(pieces[i], "panel", 1))
        outs = fore(c, pieces)
        projected.append(spread(outs))
    out = None
    for c in range(chunks):
        out = place(c, projected[c], out)
    new_volume = jnp.concatenate(new_parts, axis=0)
    return (new_volume, out)


def solution(mesh):
    in_specs = (
        P(("angle", "panel"), None, None),
        P(("angle", "panel"), None, None),
        P(),
        P(),
        P("angle", "panel"),
        P("panel", None, None),
        P("panel"),
        P("panel"),
        P("panel"),
    )
    out_specs = (P("angle", "panel"), P(("angle", "panel"), None, None))
    return jax.shard_map(
        per_device, mesh=mesh, in_specs=in_specs, out_specs=out_specs, check_vma=False
    )
```
